128 devices in a mesh: section: 2 (over core), lat: 32 (over x, y, z_lo), dp: 2 (over z_hi).
Axes of the slice: x: 4, y: 4, z: 4 (z_hi: 2, z_lo: 2; z = z_hi * 2 + z_lo), core: 2. Of those that a mesh axis runs over, the one named last changes fastest.
Arguments:
- volume: bfloat16 [8, 32, 64, 8, 256], P('dp', None, 'lat'), may hold values from -6 to 6
- cotangent: bfloat16 [8, 32, 64, 8, 256], P('dp', None, 'lat'), may hold values from -6 to 6
- weights: bfloat16 [2, 32, 32, 3, 3, 3], P('section'), may hold values from -0.21875 to 0.21875
Outputs:
- level_field: bfloat16 [2, 8, 32, 64, 8, 256], P('section', 'dp', None, 'lat')
- weight_grads: float32 [2, 32, 32, 3, 3, 3], P('section')
The draws below stay inside these ranges and needn't reach their ends.
All inputs are finite; a program needn't handle non-finite values.
Results may differ from the reference program's by a relative error of at most 0.0075.
Values may be sent and summed in bfloat16 or wider, within the bound.
No kernel may reach another device: no remote copies, remote signals or barrier semaphores. Data moves between devices by JAX's collectives and lax.ppermute only.
A program may use at most 128 MiB of HBM per device.

```python
import jax
import jax.numpy as jnp
from jax import lax

CHANNELS = 32
DEPTH = 8
BREADTH = 256
CLIPS = 8
AA = 64


def block_scale(rng, dims, cuts, smallest, largest):
    def one(axis_at, shards_of):
        heights = jax.random.uniform(jax.random.fold_in(jax.random.fold_in(rng, 6), axis_at), (shards_of,), jnp.float32, smallest / len(cuts), largest / len(cuts))
        return jnp.repeat(jnp.exp(heights), dims[axis_at] // shards_of).reshape((-1,) + (1,) * (len(dims) - axis_at - 1))

    level = one(*cuts[0])
    for cut in cuts[1:]:
        level = level * one(*cut)
    return level


def noise(key, shape, scale, bound, cuts=(), kind=jnp.bfloat16):
    result = scale * jax.random.normal(key, shape, jnp.float32)
    if cuts:
        result = result * block_scale(key, shape, cuts, -0.22, 0.18)
    return jnp.clip(result, -bound, bound).astype(kind)


def setup_inputs(seed: int = 0) -> dict:
    arg_keys = jax.random.split(jax.random.key(seed), 4)
    return {
        "volume": noise(arg_keys[0], (CLIPS, CHANNELS, AA, DEPTH, BREADTH), 1.0, 6.0, ((0, 2), (2, 32))),
        "cotangent": noise(arg_keys[1], (CLIPS, CHANNELS, AA, DEPTH, BREADTH), 1.0, 6.0, ((0, 2), (2, 32))),
        "weights": noise(arg_keys[2], (2, CHANNELS, CHANNELS, 3, 3, 3), (27 * CHANNELS) ** -0.5, 0.21875, ((0, 2),)),
    }


def apply_conv(padded, kernel):
    return lax.conv_general_dilated(padded, kernel, (1, 1, 1), ((0, 0), (1, 1), (1, 1)), dimension_numbers=('NCDHW', 'OIDHW', 'NCDHW'), preferred_element_type=jnp.float32)

def flipped(kernel):
    return jnp.transpose(jnp.flip(kernel, (2, 3, 4)), (1, 0, 2, 3, 4))

def kernel_grad(padded, delta):
    raw_grad = lax.conv_general_dilated(padded, delta, (1, 1, 1), ((0, 0), (1, 1), (1, 1)), dimension_numbers=('CNDHW', 'IODHW', 'NCDHW'), preferred_element_type=jnp.float32)
    return jnp.transpose(raw_grad, (1, 0, 2, 3, 4))

def slope(pre_act):
    sigmoid_val = jax.nn.sigmoid(pre_act)
    return sigmoid_val * (1.0 + pre_act * (1.0 - sigmoid_val))

def pad_split(field):
    return jnp.pad(field, ((0, 0), (0, 0), (1, 1), (0, 0), (0, 0)))

def reference(volume, cotangent, weights):
    kernel_zero = weights[0]
    kernel_one = weights[1]

    def one_clip(carry, pair):
        clip_in, clip_cot = pair
        field = clip_in[None]
        outer_grad = clip_cot[None]
        pad_zero = pad_split(field)
        pre_zero = apply_conv(pad_zero, kernel_zero)
        mid_field = (field.astype(jnp.float32) + jax.nn.silu(pre_zero)).astype(jnp.bfloat16)
        pad_one = pad_split(mid_field)
        pre_one = apply_conv(pad_one, kernel_one)
        top_field = (mid_field.astype(jnp.float32) + jax.nn.silu(pre_one)).astype(jnp.bfloat16)
        delta_one = (outer_grad.astype(jnp.float32) * slope(pre_one)).astype(jnp.bfloat16)
        back_mid = (outer_grad.astype(jnp.float32) + apply_conv(pad_split(delta_one), flipped(kernel_one))).astype(jnp.bfloat16)
        delta_zero = (back_mid.astype(jnp.float32) * slope(pre_zero)).astype(jnp.bfloat16)
        back_in = (back_mid.astype(jnp.float32) + apply_conv(pad_split(delta_zero), flipped(kernel_zero))).astype(jnp.bfloat16)
        carry = (carry[0] + kernel_grad(pad_zero, delta_zero), carry[1] + kernel_grad(pad_one, delta_one))
        return (carry, (back_in[0], top_field[0]))
    empty = jnp.zeros(weights.shape[1:], jnp.float32)
    grad_pair, fields = lax.scan(one_clip, (empty, empty), (volume, cotangent))
    return (jnp.stack([fields[0], fields[1]], 0), jnp.stack([grad_pair[0], grad_pair[1]], 0))
```

```python
import functools

import jax
import jax.numpy as jnp
from jax import lax
from jax.experimental import pallas as pl
from jax.experimental.pallas import tpu as pltpu
from jax.sharding import PartitionSpec as P

AXES = ("section", "lat", "dp")
BF = jnp.bfloat16
F32 = jnp.float32
VMEM_BYTES = 60 * 1024 * 1024


def permute(value, move):
    sizes = [lax.axis_size(a) for a in AXES]
    pairs = []
    for s in range(sizes[0]):
        for l in range(sizes[1]):
            for d in range(sizes[2]):
                target = move(s, l, d)
                if target is None or not 0 <= target[1] < sizes[1]:
                    continue
                source_id = (s * sizes[1] + l) * sizes[2] + d
                target_id = (target[0] * sizes[1] + target[1]) * sizes[2] + target[2]
                pairs.append((source_id, target_id))
    return lax.ppermute(value, AXES, pairs)


def lat_move(even, odd):
    return lambda s, l, d: (s, l + (odd if l % 2 else even), d)


PARTNER = lat_move(1, -1)
NEAR_CROSS = lat_move(-1, 1)
NEAR_SAME = lat_move(-2, 2)
FAR_SAME = lat_move(2, -2)
FAR_CROSS = lat_move(3, -3)


def other_section(s, l, d):
    return (1 - s, l, d)


def ring(axis, step):
    def move(s, l, d):
        at = [l // 8, (l // 2) % 4, d * 2 + l % 2]
        at[axis] = (at[axis] + step) % 4
        return (s, at[0] * 8 + at[1] * 2 + at[2] % 2, at[2] // 2)

    return move


def to_field(field, cross, flip):
    def move(s, l, d):
        if (s != field) != cross:
            return None
        return (field, l ^ 1 if flip else l, d)

    return move


def load_cell(ref, cell):
    part = ref[:, cell]
    return part.astype(F32).reshape(256, 256)


def put_stack(ref, at, value):
    lane = lax.broadcasted_iota(jnp.int32, (256, 256), 1)
    before = jnp.where(lane == 0, 0.0, pltpu.roll(value, 1, 1))
    after = jnp.where(lane == 255, 0.0, pltpu.roll(value, 255, 1))
    ref[at, 0:256] = before.astype(BF)
    ref[at, 256:512] = value.astype(BF)
    ref[at, 512:768] = after.astype(BF)


def conv_cell(mat, block, slices):
    total = None
    for p in range(3):
        term = jnp.dot(mat[block, p], slices[p], preferred_element_type=F32)
        total = term if total is None else total + term
    return total


def round_bf(value):
    return value.astype(BF).astype(F32)


def slope(value):
    sig = jax.nn.sigmoid(value)
    return sig * (1.0 + value * (1.0 - sig))


def band_kernel(w_ref, wt_ref, out_ref):
    row = lax.broadcasted_iota(jnp.int32, (256, 256), 0) % 8
    lane = lax.broadcasted_iota(jnp.int32, (256, 256), 1) % 8
    gap = lane - row
    spread = jnp.where(
        lax.broadcasted_iota(jnp.int32, (32, 256), 1) // 8
        == lax.broadcasted_iota(jnp.int32, (32, 256), 0),
        1.0,
        0.0,
    ).astype(BF)
    tall = jnp.where(
        lax.broadcasted_iota(jnp.int32, (256, 32), 0) // 8
        == lax.broadcasted_iota(jnp.int32, (256, 32), 1),
        1.0,
        0.0,
    ).astype(BF)
    for block in range(2):
        for back in range(2):
            src = wt_ref if back else w_ref
            wide = jnp.dot(
                src[block].reshape(864, 32), spread, preferred_element_type=F32
            ).astype(BF)
            for p in range(3):
                for r in range(3):
                    mat = jnp.zeros((256, 256), F32)
                    for q in range(3):
                        n = (p * 3 + q) * 3 + r
                        if back:
                            n = 26 - n
                        full = jnp.dot(
                            tall, wide[32 * n : 32 * n + 32], preferred_element_type=F32
                        )
                        mat = jnp.where(gap == q - 1, full, mat)
                    out_ref[2 * block + back, p, :, 256 * r : 256 * r + 256] = mat.astype(BF)


def make_bands(w, wt):
    return pl.pallas_call(
        band_kernel,
        out_shape=jax.ShapeDtypeStruct((4, 3, 256, 768), BF),
        compiler_params=pltpu.CompilerParams(vmem_limit_bytes=VMEM_BYTES),
        name="bands",
    )(w, wt)


def valid_cell(at, pair, pairs):
    if at < 0:
        return pair > 0
    if at >= 4:
        return pair < pairs - 1
    return None


def masked(value, at, pair, pairs):
    ok = valid_cell(at, pair, pairs)
    return value if ok is None else jnp.where(ok, value, 0.0)


def pick_slab(refs, z):
    own, partner, nc, ns, fc, fs = refs
    return [(fs, fc), (nc, ns), (own, partner), (partner, own), (ns, nc), (fc, fs)]


def forward_kernel(pairs, pos_ref, own, partner, nc, ns, fc, fs, mat,
                   xv_ref, xm_ref, pre0_ref, pre1_ref, top_own, top_oth, xv_s, xm_s):
    z = pos_ref[0]
    pair = pos_ref[1]
    even = z == 0
    slabs = pick_slab((own, partner, nc, ns, fc, fs), z)

    def xv(a):
        return (xv_ref, a + 1) if -1 <= a < 5 else (xv_s, a + 4 if a < -1 else a - 2)

    def xm(a):
        return (xm_ref, a + 1) if -1 <= a < 5 else (xm_s, a + 3 if a < -1 else a - 3)

    for a in range(-4, 8):
        j = a + 4
        first, second = slabs[j // 2]
        value = jnp.where(even, load_cell(first, j % 2), load_cell(second, j % 2))
        ref, at = xv(a)
        put_stack(ref, at, value)
    for a in range(-3, 7):
        near = [xv(a + p - 1) for p in range(3)]
        pre = conv_cell(mat, 0, [ref[at] for ref, at in near])
        if -1 <= a < 5:
            pre0_ref[a + 1] = pre
        field = near[1][0][near[1][1], 256:512].astype(F32)
        mid = round_bf(field + pre * jax.nn.sigmoid(pre))
        ref, at = xm(a)
        put_stack(ref, at, masked(mid, a, pair, pairs))
    for a in range(-2, 6):
        near = [xm(a + p - 1) for p in range(3)]
        pre = conv_cell(mat, 2, [ref[at] for ref, at in near])
        pre1_ref[a + 2] = pre
        if 0 <= a < 4:
            mid = near[1][0][near[1][1], 256:512].astype(F32)
            top = (mid + pre * jax.nn.sigmoid(pre)).reshape(32, 8, 256).astype(BF)
            mine = even if a < 2 else jnp.logical_not(even)

            @pl.when(mine)
            def _():
                top_own[:, a % 2] = top

            @pl.when(jnp.logical_not(mine))
            def _():
                top_oth[:, a % 2] = top


VM = pl.BlockSpec(memory_space=pltpu.MemorySpace.VMEM)
SM = pl.BlockSpec(memory_space=pltpu.MemorySpace.SMEM)
SLAB = jax.ShapeDtypeStruct((32, 2, 8, 256), BF)
STACK = jax.ShapeDtypeStruct((6, 768, 256), BF)


def run_forward(pairs, pos, slabs, mats):
    return pl.pallas_call(
        functools.partial(forward_kernel, pairs),
        in_specs=[SM] + [VM] * 7,
        out_specs=[VM] * 6,
        out_shape=[
            STACK,
            STACK,
            jax.ShapeDtypeStruct((6, 256, 256), F32),
            jax.ShapeDtypeStruct((8, 256, 256), F32),
            SLAB,
            SLAB,
        ],
        scratch_shapes=[pltpu.VMEM((6, 768, 256), BF), pltpu.VMEM((4, 768, 256), BF)],
        compiler_params=pltpu.CompilerParams(vmem_limit_bytes=VMEM_BYTES),
        name="forward",
    )(pos, *slabs, mats)


def kernel_grad(delta_ref, x_ref, store):
    delta = jnp.concatenate([delta_ref(a) for a in range(4)], axis=1)
    row = lax.broadcasted_iota(jnp.int32, (256, 256), 0) % 8
    lane = lax.broadcasted_iota(jnp.int32, (256, 256), 1) % 8
    gap = lane - row
    fold_row = lax.broadcasted_iota(jnp.int32, (2048, 128), 0)
    fold_lane = lax.broadcasted_iota(jnp.int32, (2048, 128), 1)
    fold = jnp.where((fold_row % 1024) // 8 == fold_lane, 1.0, 0.0).astype(BF)
    parts = {}
    for p in range(3):
        field = jnp.concatenate([x_ref[a + p] for a in range(4)], axis=1)
        full = lax.dot_general(
            delta, field, (((1,), (1,)), ((), ())), preferred_element_type=F32
        )
        for r in range(3):
            piece = full[:, 256 * r : 256 * r + 256]
            for q in range(3):
                parts[(p * 3 + q) * 3 + r] = jnp.where(gap == q - 1, piece, 0.0)
        for u in range(7):
            members = [n for n in range(4 * u, 4 * u + 4) if n < 27]
            if not all(n in parts for n in members) or max(members) < 9 * p:
                continue
            high = []
            low = []
            for n in range(4 * u, 4 * u + 4):
                if n < 27:
                    part = parts[n]
                    top = part.astype(BF)
                    high.append(top)
                    low.append((part - top.astype(F32)).astype(BF))
                else:
                    high.append(jnp.zeros((256, 256), BF))
                    low.append(jnp.zeros((256, 256), BF))
            summed = jnp.dot(
                jnp.concatenate(high + low, axis=1), fold, preferred_element_type=F32
            )
            store(u, summed.reshape(32, 8, 128).sum(axis=1))


def backward_kernel(pairs, pos_ref, own, partner, nc, ns, mat, xv_ref, xm_ref, pre0_ref,
                    pre1_ref, xd0_ref, bm_ref, keep_ref, send_ref, xd1_s, bmh_s, cot_s):
    z = pos_ref[0]
    pair = pos_ref[1]
    even = z == 0
    zero_section = pos_ref[2] == 0
    slabs = [(nc, ns), (own, partner), (partner, own), (ns, nc)]
    for a in range(-2, 6):
        j = a + 2
        first, second = slabs[j // 2]
        cot = jnp.where(even, load_cell(first, j % 2), load_cell(second, j % 2))
        put_stack(xd1_s, j, round_bf(cot * slope(pre1_ref[j])))
        if -1 <= a < 5:
            cot_s[a + 1] = cot
    for a in range(-1, 5):
        pre = conv_cell(mat, 3, [xd1_s[a + 2 + p - 1] for p in range(3)])
        back = round_bf(cot_s[a + 1] + pre)
        if 0 <= a < 4:
            bm_ref[a] = back.astype(BF)
        delta = round_bf(back * slope(pre0_ref[a + 1]))
        put_stack(xd0_ref, a + 1, masked(delta, a, pair, pairs))

    def store_zero(u, value):
        rows = slice(32 * u, 32 * u + 32)

        @pl.when(zero_section)
        def _():
            keep_ref[rows] = value

        @pl.when(jnp.logical_not(zero_section))
        def _():
            send_ref[rows] = value

    def store_one(u, value):
        rows = slice(32 * u, 32 * u + 32)

        @pl.when(zero_section)
        def _():
            send_ref[rows] = value

        @pl.when(jnp.logical_not(zero_section))
        def _():
            keep_ref[rows] = value

    kernel_grad(lambda a: xd0_ref[a + 1, 256:512], xv_ref, store_zero)
    kernel_grad(lambda a: xd1_s[a + 2, 256:512], xm_ref, store_one)


def run_backward(pairs, pos, slabs, mats, xv, xm, pre0, pre1):
    grad = jax.ShapeDtypeStruct((224, 128), F32)
    return pl.pallas_call(
        functools.partial(backward_kernel, pairs),
        in_specs=[SM] + [VM] * 9,
        out_specs=[VM] * 4,
        out_shape=[STACK, jax.ShapeDtypeStruct((4, 256, 256), BF), grad, grad],
        scratch_shapes=[
            pltpu.VMEM((8, 768, 256), BF),
            pltpu.VMEM((1, 8, 128), F32),
            pltpu.VMEM((6, 256, 256), F32),
        ],
        compiler_params=pltpu.CompilerParams(vmem_limit_bytes=VMEM_BYTES),
        name="backward",
    )(pos, *slabs, mats, xv, xm, pre0, pre1)


def last_kernel(pos_ref, xd0_ref, bm_ref, mat, out_own, out_oth):
    even = pos_ref[0] == 0
    for a in range(4):
        pre = conv_cell(mat, 1, [xd0_ref[a + p] for p in range(3)])
        out = (bm_ref[a].astype(F32) + pre).reshape(32, 8, 256).astype(BF)
        mine = even if a < 2 else jnp.logical_not(even)

        @pl.when(mine)
        def _():
            out_own[:, a % 2] = out

        @pl.when(jnp.logical_not(mine))
        def _():
            out_oth[:, a % 2] = out


def run_last(pos, xd0, bm, mats):
    return pl.pallas_call(
        last_kernel,
        in_specs=[SM] + [VM] * 3,
        out_specs=[VM] * 2,
        out_shape=[SLAB, SLAB],
        compiler_params=pltpu.CompilerParams(vmem_limit_bytes=VMEM_BYTES),
        name="last",
    )(pos, xd0, bm, mats)


def gather_kernel(pos_ref, *refs):
    pieces, (out_ref, sems) = refs[:8], refs[8:]
    z = pos_ref[0]
    s = pos_ref[2]
    for field in range(2):
        @pl.when(s == field)
        def _():
            copies = []
            for n in range(4):
                clip = 2 * (s ^ (n // 2)) + (z ^ (n % 2))
                copies.append(
                    pltpu.make_async_copy(
                        pieces[4 * field + n], out_ref.at[clip], sems.at[n]
                    )
                )
            for copy in copies:
                copy.start()
            for copy in copies:
                copy.wait()


def run_gather(pos, pieces):
    hbm = pl.BlockSpec(memory_space=pl.ANY)
    return pl.pallas_call(
        gather_kernel,
        in_specs=[SM] + [hbm] * 8,
        out_specs=hbm,
        out_shape=jax.ShapeDtypeStruct((4, 32, 2, 8, 256), BF),
        scratch_shapes=[pltpu.SemaphoreType.DMA((4,))],
        name="gather",
    )(pos, *pieces)


def unfold_kernel(in_ref, out_ref):
    for n in range(27):
        u, g = divmod(n, 4)
        out_ref[n] = in_ref[32 * u : 32 * u + 32, 32 * g : 32 * g + 32]


def run_unfold(grads):
    return pl.pallas_call(
        unfold_kernel,
        out_shape=jax.ShapeDtypeStruct((27, 32, 32), F32),
        name="unfold",
    )(grads)


def body(volume, cotangent, weights):
    s = lax.axis_index("section")
    l = lax.axis_index("lat")
    pairs = lax.axis_size("lat") // 2
    z = l % 2
    pos = jnp.stack([z, l // 2, s]).astype(jnp.int32)

    def clip(array, at):
        return lax.dynamic_index_in_dim(array, at, 0, keepdims=False)

    same = 2 * s + z
    cross = 2 * s + (1 - z)
    mine = jnp.transpose(weights[0], (2, 3, 4, 0, 1)).reshape(27, 32, 32)
    others = permute(mine, other_section)
    v_same, v_cross = clip(volume, same), clip(volume, cross)
    v_slabs = [
        v_same,
        permute(v_cross, PARTNER),
        permute(v_cross, NEAR_CROSS),
        permute(v_same, NEAR_SAME),
        permute(v_cross, FAR_CROSS),
        permute(v_same, FAR_SAME),
    ]
    c_same, c_cross = clip(cotangent, same), clip(cotangent, cross)
    c_slabs = [
        c_same,
        permute(c_cross, PARTNER),
        permute(c_cross, NEAR_CROSS),
        permute(c_same, NEAR_SAME),
    ]
    both = jnp.where(
        s == 0, jnp.stack([mine, others]), jnp.stack([others, mine])
    )
    mats = make_bands(both, jnp.swapaxes(both, 2, 3))
    xv, xm, pre0, pre1, top_own, top_oth = run_forward(pairs, pos, v_slabs, mats)
    top_pieces = [
        top_own,
        permute(top_oth, to_field(1, False, True)),
        permute(top_own, to_field(1, True, False)),
        permute(top_oth, to_field(1, True, True)),
    ]
    xd0, bm, keep, send = run_backward(pairs, pos, c_slabs, mats, xv, xm, pre0, pre1)
    out_own, out_oth = run_last(pos, xd0, bm, mats)
    out_pieces = [
        out_own,
        permute(out_oth, to_field(0, False, True)),
        permute(out_own, to_field(0, True, False)),
        permute(out_oth, to_field(0, True, True)),
    ]
    total = keep + permute(send, other_section)
    for axis in (2, 1, 0):
        total = (total + permute(total, ring(axis, 2))) + (
            permute(total, ring(axis, 1)) + permute(total, ring(axis, 3))
        )
    field = run_gather(pos, out_pieces + top_pieces)
    grads = run_unfold(total).reshape(3, 3, 3, 32, 32)
    return (field[None], jnp.transpose(grads, (3, 4, 0, 1, 2))[None])


def solution(mesh):
    return jax.shard_map(
        body,
        mesh=mesh,
        in_specs=(
            P("dp", None, "lat", None, None),
            P("dp", None, "lat", None, None),
            P("section", None, None, None, None, None),
        ),
        out_specs=(
            P("section", "dp", None, "lat", None, None),
            P("section", None, None, None, None, None),
        ),
        check_vma=False,
    )
```

```python
import functools

import jax
import jax.numpy as jnp
from jax import lax
from jax.experimental import pallas as pl
from jax.experimental.pallas import tpu as pltpu
from jax.sharding import PartitionSpec as P

AXES = ("section", "lat", "dp")
BF = jnp.bfloat16
F32 = jnp.float32
VMEM_BYTES = 20 * 1024 * 1024


def permute(value, move):
    sizes = [lax.axis_size(a) for a in AXES]
    pairs = []
    for s in range(sizes[0]):
        for l in range(sizes[1]):
            for d in range(sizes[2]):
                target = move(s, l, d)
                if target is None or not 0 <= target[1] < sizes[1]:
                    continue
                source_id = (s * sizes[1] + l) * sizes[2] + d
                target_id = (target[0] * sizes[1] + target[1]) * sizes[2] + target[2]
                pairs.append((source_id, target_id))
    return lax.ppermute(value, AXES, pairs)


def lat_move(even, odd):
    return lambda s, l, d: (s, l + (odd if l % 2 else even), d)


PARTNER = lat_move(1, -1)
NEAR_CROSS = lat_move(-1, 1)
NEAR_SAME = lat_move(-2, 2)
FAR_SAME = lat_move(2, -2)
FAR_CROSS = lat_move(3, -3)


def other_section(s, l, d):
    return (1 - s, l, d)


def ring(axis, step):
    def move(s, l, d):
        at = [l // 8, (l // 2) % 4, d * 2 + l % 2]
        at[axis] = (at[axis] + step) % 4
        return (s, at[0] * 8 + at[1] * 2 + at[2] % 2, at[2] // 2)

    return move


def other_both(s, l, d):
    return (1 - s, l ^ 1, d)


def load_cell(ref, plane, cell):
    part = ref[plane, :, cell]
    return part.astype(F32).reshape(256, 256)


def put_stack(ref, at, value):
    lane = lax.broadcasted_iota(jnp.int32, (256, 256), 1)
    before = jnp.where(lane == 0, 0.0, pltpu.roll(value, 1, 1))
    after = jnp.where(lane == 255, 0.0, pltpu.roll(value, 255, 1))
    ref[at, 0:256] = before.astype(BF)
    ref[at, 256:512] = value.astype(BF)
    ref[at, 512:768] = after.astype(BF)


def conv_cell(mat, slices):
    total = None
    for p in range(3):
        term = jnp.dot(mat[p], slices[p], preferred_element_type=F32)
        total = term if total is None else total + term
    return total


def round_bf(value):
    return value.astype(BF).astype(F32)


def slope(value):
    sig = jax.nn.sigmoid(value)
    return sig * (1.0 + value * (1.0 - sig))


def band_kernel(w_ref, wt_ref, *out_refs):
    row = lax.broadcasted_iota(jnp.int32, (256, 256), 0) % 8
    lane = lax.broadcasted_iota(jnp.int32, (256, 256), 1) % 8
    gap = lane - row
    spread = jnp.where(
        lax.broadcasted_iota(jnp.int32, (32, 256), 1) // 8
        == lax.broadcasted_iota(jnp.int32, (32, 256), 0),
        1.0,
        0.0,
    ).astype(BF)
    tall = jnp.where(
        lax.broadcasted_iota(jnp.int32, (256, 32), 0) // 8
        == lax.broadcasted_iota(jnp.int32, (256, 32), 1),
        1.0,
        0.0,
    ).astype(BF)
    for block in range(2):
        for back in range(2):
            src = wt_ref if back else w_ref
            wide = jnp.dot(
                src[block].reshape(864, 32), spread, preferred_element_type=F32
            ).astype(BF)
            for p in range(3):
                for r in range(3):
                    mat = jnp.zeros((256, 256), F32)
                    for q in range(3):
                        n = (p * 3 + q) * 3 + r
                        if back:
                            n = 26 - n
                        full = jnp.dot(
                            tall, wide[32 * n : 32 * n + 32], preferred_element_type=F32
                        )
                        mat = jnp.where(gap == q - 1, full, mat)
                    out_refs[2 * block + back][p, :, 256 * r : 256 * r + 256] = mat.astype(BF)


def make_bands(w, wt):
    return pl.pallas_call(
        band_kernel,
        out_shape=[jax.ShapeDtypeStruct((3, 256, 768), BF)] * 4,
        compiler_params=pltpu.CompilerParams(vmem_limit_bytes=VMEM_BYTES),
        name="bands",
    )(w, wt)


def valid_cell(at, pair, pairs):
    if at < 0:
        return pair > 0
    if at >= 4:
        return pair < pairs - 1
    return None


def masked(value, at, pair, pairs):
    ok = valid_cell(at, pair, pairs)
    return value if ok is None else jnp.where(ok, value, 0.0)


def pick_slab(refs, z):
    own, partner, nc, ns, fc, fs = refs
    return [(fs, fc), (nc, ns), (own, partner), (partner, own), (ns, nc), (fc, fs)]


def forward_kernel(pairs, pos_ref, own, partner, nc, ns, fc, fs, mat0, mat1,
                   xv_ref, xm_ref, pre0_ref, pre1_ref, top_own, top_oth, xv_s, xm_s):
    z = pos_ref[0]
    pair = pos_ref[1]
    even = z == 0
    slabs = pick_slab((own, partner, nc, ns, fc, fs), z)

    def xv(a):
        return (xv_ref, a + 1) if -1 <= a < 5 else (xv_s, a + 4 if a < -1 else a - 2)

    def xm(a):
        return (xm_ref, a + 1) if -1 <= a < 5 else (xm_s, a + 3 if a < -1 else a - 3)

    for a in range(-4, 8):
        j = a + 4
        first, second = slabs[j // 2]
        value = jnp.where(even, load_cell(first, 0, j % 2), load_cell(second, 0, j % 2))
        ref, at = xv(a)
        put_stack(ref, at, value)
    for a in range(-3, 7):
        near = [xv(a + p - 1) for p in range(3)]
        pre = conv_cell(mat0, [ref[at] for ref, at in near])
        if -1 <= a < 5:
            pre0_ref[a + 1] = pre
        field = near[1][0][near[1][1], 256:512].astype(F32)
        mid = round_bf(field + pre * jax.nn.sigmoid(pre))
        ref, at = xm(a)
        put_stack(ref, at, masked(mid, a, pair, pairs))
    for a in range(-2, 6):
        near = [xm(a + p - 1) for p in range(3)]
        pre = conv_cell(mat1, [ref[at] for ref, at in near])
        pre1_ref[a + 2] = pre
        if 0 <= a < 4:
            mid = near[1][0][near[1][1], 256:512].astype(F32)
            top = (mid + pre * jax.nn.sigmoid(pre)).reshape(32, 8, 256).astype(BF)
            mine = even if a < 2 else jnp.logical_not(even)

            @pl.when(mine)
            def _():
                top_own[:, a % 2] = top

            @pl.when(jnp.logical_not(mine))
            def _():
                top_oth[:, a % 2] = top


VM = pl.BlockSpec(memory_space=pltpu.MemorySpace.VMEM)
SM = pl.BlockSpec(memory_space=pltpu.MemorySpace.SMEM)
SLAB = jax.ShapeDtypeStruct((32, 2, 8, 256), BF)
STACK = jax.ShapeDtypeStruct((6, 768, 256), BF)


def run_forward(pairs, pos, slabs, mat0, mat1):
    return pl.pallas_call(
        functools.partial(forward_kernel, pairs),
        in_specs=[SM] + [VM] * 8,
        out_specs=[VM] * 6,
        out_shape=[
            STACK,
            STACK,
            jax.ShapeDtypeStruct((6, 256, 256), F32),
            jax.ShapeDtypeStruct((8, 256, 256), F32),
            SLAB,
            SLAB,
        ],
        scratch_shapes=[pltpu.VMEM((6, 768, 256), BF), pltpu.VMEM((4, 768, 256), BF)],
        compiler_params=pltpu.CompilerParams(vmem_limit_bytes=VMEM_BYTES),
        name="forward",
    )(pos, *slabs, mat0, mat1)


def kernel_grad(delta_ref, x_ref, scr, keep_ref, send_ref, kept):
    delta = jnp.concatenate([delta_ref(a) for a in range(4)], axis=1)
    for p in range(3):
        field = jnp.concatenate([x_ref[a + p] for a in range(4)], axis=1)
        full = lax.dot_general(
            delta, field, (((1,), (1,)), ((), ())), preferred_element_type=F32
        )
        for t in range(6):
            scr[6 * p + t] = full[:, 128 * t : 128 * t + 128]
    lane_row = lax.broadcasted_iota(jnp.int32, (256, 128), 0)
    fold_lane = lax.broadcasted_iota(jnp.int32, (256, 128), 1)
    total = None
    for d in range(8):
        rows = jnp.concatenate(
            [
                jnp.concatenate(
                    [scr[2 * n + t, pl.ds(d, 32, stride=8), :] for t in range(2)], axis=1
                )
                for n in range(9)
            ],
            axis=0,
        )
        high = rows.astype(BF)
        low = (rows - high.astype(F32)).astype(BF)
        fold = jnp.where(
            ((lane_row // 8) == (fold_lane % 32))
            & ((lane_row % 8) == d - 1 + fold_lane // 32)
            & (fold_lane < 96),
            1.0,
            0.0,
        ).astype(BF)
        term = jnp.dot(high, fold, preferred_element_type=F32) + jnp.dot(
            low, fold, preferred_element_type=F32
        )
        total = term if total is None else total + term

    @pl.when(kept)
    def _():
        keep_ref[...] = total

    @pl.when(jnp.logical_not(kept))
    def _():
        send_ref[...] = total


def backward_kernel(pairs, pos_ref, own, partner, nc, ns, mat, xv_ref, xm_ref, pre0_ref,
                    pre1_ref, xd0_ref, bm_ref, keep_ref, send_ref, xd1_s, scr, cot_s):
    z = pos_ref[0]
    pair = pos_ref[1]
    even = z == 0
    zero_section = pos_ref[2] == 0
    slabs = [(nc, ns), (own, partner), (partner, own), (ns, nc)]
    for a in range(-2, 6):
        j = a + 2
        first, second = slabs[j // 2]
        cot = jnp.where(even, load_cell(first, 1, j % 2), load_cell(second, 1, j % 2))
        put_stack(xd1_s, j, round_bf(cot * slope(pre1_ref[j])))
        if -1 <= a < 5:
            cot_s[a + 1] = cot
    for a in range(-1, 5):
        pre = conv_cell(mat, [xd1_s[a + 2 + p - 1] for p in range(3)])
        back = round_bf(cot_s[a + 1] + pre)
        if 0 <= a < 4:
            bm_ref[a] = back.astype(BF)
        delta = round_bf(back * slope(pre0_ref[a + 1]))
        put_stack(xd0_ref, a + 1, masked(delta, a, pair, pairs))

    kernel_grad(
        lambda a: xd0_ref[a + 1, 256:512], xv_ref, scr, keep_ref, send_ref, zero_section
    )
    kernel_grad(
        lambda a: xd1_s[a + 2, 256:512], xm_ref, scr, keep_ref, send_ref,
        jnp.logical_not(zero_section),
    )


def run_backward(pairs, pos, slabs, mats, xv, xm, pre0, pre1):
    grad = jax.ShapeDtypeStruct((288, 128), F32)
    return pl.pallas_call(
        functools.partial(backward_kernel, pairs),
        in_specs=[SM] + [VM] * 9,
        out_specs=[VM] * 4,
        out_shape=[STACK, jax.ShapeDtypeStruct((4, 256, 256), BF), grad, grad],
        scratch_shapes=[
            pltpu.VMEM((8, 768, 256), BF),
            pltpu.VMEM((18, 256, 128), F32),
            pltpu.VMEM((6, 256, 256), F32),
        ],
        compiler_params=pltpu.CompilerParams(vmem_limit_bytes=VMEM_BYTES),
        name="backward",
    )(pos, *slabs, mats, xv, xm, pre0, pre1)


def last_kernel(pos_ref, xd0_ref, bm_ref, mat, out_own, out_oth):
    even = pos_ref[0] == 0
    for a in range(4):
        pre = conv_cell(mat, [xd0_ref[a + p] for p in range(3)])
        out = (bm_ref[a].astype(F32) + pre).reshape(32, 8, 256).astype(BF)
        mine = even if a < 2 else jnp.logical_not(even)

        @pl.when(mine)
        def _():
            out_own[:, a % 2] = out

        @pl.when(jnp.logical_not(mine))
        def _():
            out_oth[:, a % 2] = out


def run_last(pos, xd0, bm, mats):
    return pl.pallas_call(
        last_kernel,
        in_specs=[SM] + [VM] * 3,
        out_specs=[VM] * 2,
        out_shape=[SLAB, SLAB],
        compiler_params=pltpu.CompilerParams(vmem_limit_bytes=VMEM_BYTES),
        name="last",
    )(pos, xd0, bm, mats)


def gather_kernel(pos_ref, own0, own1, part, sec, both, out_ref, sems):
    z = pos_ref[0]
    s = pos_ref[2]

    def piece(n, ref):
        clip = 2 * (s ^ (n // 2)) + (z ^ (n % 2))
        return pltpu.make_async_copy(ref, out_ref.at[clip], sems.at[n])

    @pl.when(s == 0)
    def _():
        piece(0, own0).start()

    @pl.when(s == 1)
    def _():
        piece(0, own1).start()

    for n, ref in ((1, part), (2, sec), (3, both)):
        piece(n, ref).start()
    for n, ref in ((0, own0), (1, part), (2, sec), (3, both)):
        piece(n, ref).wait()


def run_gather(pos, pieces):
    return pl.pallas_call(
        gather_kernel,
        in_specs=[SM] + [VM] * 5,
        out_specs=pl.BlockSpec(memory_space=pl.ANY),
        out_shape=jax.ShapeDtypeStruct((4, 32, 2, 8, 256), BF),
        scratch_shapes=[pltpu.SemaphoreType.DMA((4,))],
        compiler_params=pltpu.CompilerParams(vmem_limit_bytes=VMEM_BYTES),
        name="gather",
    )(pos, *pieces)


def unfold_kernel(a_ref, b_ref, c_ref, d_ref, out_ref):
    for n in range(9):
        rows = slice(32 * n, 32 * n + 32)
        value = (a_ref[rows] + b_ref[rows]) + (c_ref[rows] + d_ref[rows])
        p, r = divmod(n, 3)
        for q in range(3):
            out_ref[(p * 3 + q) * 3 + r] = value[:, 32 * q : 32 * q + 32]


def run_unfold(parts):
    return pl.pallas_call(
        unfold_kernel,
        out_shape=jax.ShapeDtypeStruct((27, 32, 32), F32),
        compiler_params=pltpu.CompilerParams(vmem_limit_bytes=VMEM_BYTES),
        name="unfold",
    )(*parts)


def body(volume, cotangent, weights):
    s = lax.axis_index("section")
    l = lax.axis_index("lat")
    pairs = lax.axis_size("lat") // 2
    z = l % 2
    pos = jnp.stack([z, l // 2, s]).astype(jnp.int32)

    def clip(array, at):
        return lax.dynamic_index_in_dim(array, at, 0, keepdims=False)

    same = 2 * s + z
    cross = 2 * s + (1 - z)
    mine = jnp.transpose(weights[0], (2, 3, 4, 0, 1)).reshape(27, 32, 32)
    others = permute(mine, other_section)
    same_vc = jnp.stack([clip(volume, same), clip(cotangent, same)])
    cross_vc = jnp.stack([clip(volume, cross), clip(cotangent, cross)])
    slabs = [
        same_vc,
        permute(cross_vc, PARTNER),
        permute(cross_vc, NEAR_CROSS),
        permute(same_vc, NEAR_SAME),
        permute(cross_vc[0:1], FAR_CROSS),
        permute(same_vc[0:1], FAR_SAME),
    ]
    both = jnp.where(
        s == 0, jnp.stack([mine, others]), jnp.stack([others, mine])
    )
    fwd0, bwd0, fwd1, bwd1 = make_bands(both, jnp.swapaxes(both, 2, 3))
    xv, xm, pre0, pre1, top_own, top_oth = run_forward(pairs, pos, slabs, fwd0, fwd1)
    xd0, bm, keep, send = run_backward(pairs, pos, slabs[:4], bwd1, xv, xm, pre0, pre1)
    out_own, out_oth = run_last(pos, xd0, bm, bwd0)
    total = keep + permute(send, other_section)
    for axis in (2, 1, 0):
        parts = [total] + [permute(total, ring(axis, step)) for step in (2, 1, 3)]
        if axis:
            total = (parts[0] + parts[1]) + (parts[2] + parts[3])
    at_zero = s == 0
    pieces = [
        out_own,
        top_own,
        permute(jnp.where(at_zero, out_oth, top_oth), PARTNER),
        permute(jnp.where(at_zero, top_own, out_own), other_section),
        permute(jnp.where(at_zero, top_oth, out_oth), other_both),
    ]
    field = run_gather(pos, pieces)
    grads = run_unfold(parts).reshape(3, 3, 3, 32, 32)
    return (field[None], jnp.transpose(grads, (3, 4, 0, 1, 2))[None])


def solution(mesh):
    return jax.shard_map(
        body,
        mesh=mesh,
        in_specs=(
            P("dp", None, "lat", None, None),
            P("dp", None, "lat", None, None),
            P("section", None, None, None, None, None),
        ),
        out_specs=(
            P("section", "dp", None, "lat", None, None),
            P("section", None, None, None, None, None),
        ),
        check_vma=False,
    )
```

```python
import functools

import jax
import jax.numpy as jnp
from jax import lax
from jax.experimental import pallas as pl
from jax.experimental.pallas import tpu as pltpu
from jax.sharding import PartitionSpec as P

AXES = ("section", "lat", "dp")
BF = jnp.bfloat16
F32 = jnp.float32
MIB = 1024 * 1024
VM = pl.BlockSpec(memory_space=pltpu.MemorySpace.VMEM)
SM = pl.BlockSpec(memory_space=pltpu.MemorySpace.SMEM)


def permute(value, move):
    sizes = [lax.axis_size(a) for a in AXES]
    pairs = []
    for s in range(sizes[0]):
        for l in range(sizes[1]):
            for d in range(sizes[2]):
                target = move(s, l, d)
                if target is None or not 0 <= target[1] < sizes[1]:
                    continue
                source_id = (s * sizes[1] + l) * sizes[2] + d
                target_id = (target[0] * sizes[1] + target[1]) * sizes[2] + target[2]
                pairs.append((source_id, target_id))
    return lax.ppermute(value, AXES, pairs)


def lat_move(even, odd):
    return lambda s, l, d: (s, l + (odd if l % 2 else even), d)


PARTNER = lat_move(1, -1)
NEAR_CROSS = lat_move(-1, 1)
NEAR_SAME = lat_move(-2, 2)
FAR_SAME = lat_move(2, -2)
FAR_CROSS = lat_move(3, -3)


def other_section(s, l, d):
    return (1 - s, l, d)


def ring(axis, step):
    def move(s, l, d):
        at = [l // 8, (l // 2) % 4, d * 2 + l % 2]
        at[axis] = (at[axis] + step) % 4
        return (s, at[0] * 8 + at[1] * 2 + at[2] % 2, at[2] // 2)

    return move


def other_both(s, l, d):
    return (1 - s, l ^ 1, d)


def load_cell(ref, cell):
    part = ref[:, cell]
    return part.astype(F32).reshape(256, 256)


def put_stack(ref, at, value):
    lane = lax.broadcasted_iota(jnp.int32, (256, 256), 1)
    before = jnp.where(lane == 0, 0.0, pltpu.roll(value, 1, 1))
    after = jnp.where(lane == 255, 0.0, pltpu.roll(value, 255, 1))
    ref[at, 0:256] = before.astype(BF)
    ref[at, 256:512] = value.astype(BF)
    ref[at, 512:768] = after.astype(BF)


def conv_cell(mat, block, slices):
    total = None
    for p in range(3):
        term = jnp.dot(mat[block, p], slices[p], preferred_element_type=F32)
        total = term if total is None else total + term
    return total


def round_bf(value):
    return value.astype(BF).astype(F32)


def slope(value):
    sig = jax.nn.sigmoid(value)
    return sig * (1.0 + value * (1.0 - sig))


def band_kernel(pos_ref, mine_ref, others_ref, fwd_ref, bwd_ref):
    row = lax.broadcasted_iota(jnp.int32, (256, 256), 0) % 8
    lane = lax.broadcasted_iota(jnp.int32, (256, 256), 1) % 8
    gap = lane - row
    spread = jnp.where(
        lax.broadcasted_iota(jnp.int32, (32, 256), 1) // 8
        == lax.broadcasted_iota(jnp.int32, (32, 256), 0),
        1.0,
        0.0,
    ).astype(BF)
    tall = jnp.where(
        lax.broadcasted_iota(jnp.int32, (256, 32), 0) // 8
        == lax.broadcasted_iota(jnp.int32, (256, 32), 1),
        1.0,
        0.0,
    ).astype(BF)
    for src, block in ((mine_ref, pos_ref[2]), (others_ref, 1 - pos_ref[2])):
        for back in range(2):
            out_ref = bwd_ref if back else fwd_ref
            wide = jnp.dot(
                src[back].reshape(864, 32), spread, preferred_element_type=F32
            ).astype(BF)
            for p in range(3):
                for r in range(3):
                    mat = jnp.zeros((256, 256), F32)
                    for q in range(3):
                        n = (p * 3 + q) * 3 + r
                        if back:
                            n = 26 - n
                        full = jnp.dot(
                            tall, wide[32 * n : 32 * n + 32], preferred_element_type=F32
                        )
                        mat = jnp.where(gap == q - 1, full, mat)
                    out_ref[block, p, :, 256 * r : 256 * r + 256] = mat.astype(BF)


def make_bands(pos, mine, others):
    return pl.pallas_call(
        band_kernel,
        in_specs=[SM, VM, VM],
        out_specs=[VM, VM],
        out_shape=[jax.ShapeDtypeStruct((2, 3, 256, 768), BF)] * 2,
        compiler_params=pltpu.CompilerParams(vmem_limit_bytes=8 * MIB),
        name="bands",
    )(pos, mine, others)


def valid_cell(at, pair, pairs):
    if at < 0:
        return pair > 0
    if at >= 4:
        return pair < pairs - 1
    return None


def masked(value, at, pair, pairs):
    ok = valid_cell(at, pair, pairs)
    return value if ok is None else jnp.where(ok, value, 0.0)


def pick_slab(refs, z):
    own, partner, nc, ns, fc, fs = refs
    return [(fs, fc), (nc, ns), (own, partner), (partner, own), (ns, nc), (fc, fs)]


def forward_kernel(pairs, pos_ref, own, partner, nc, ns, fc, fs, mat,
                   xv_ref, xm_ref, pre0_ref, pre1_ref, top_own, top_oth, xv_s, xm_s):
    z = pos_ref[0]
    pair = pos_ref[1]
    even = z == 0
    slabs = pick_slab((own, partner, nc, ns, fc, fs), z)

    def xv(a):
        return (xv_ref, a + 1) if -1 <= a < 5 else (xv_s, a + 4 if a < -1 else a - 2)

    def xm(a):
        return (xm_ref, a + 1) if -1 <= a < 5 else (xm_s, a + 3 if a < -1 else a - 3)

    for a in range(-4, 8):
        j = a + 4
        first, second = slabs[j // 2]
        value = jnp.where(even, load_cell(first, j % 2), load_cell(second, j % 2))
        ref, at = xv(a)
        put_stack(ref, at, value)
    for a in range(-3, 7):
        near = [xv(a + p - 1) for p in range(3)]
        pre = conv_cell(mat, 0, [ref[at] for ref, at in near])
        if -1 <= a < 5:
            pre0_ref[a + 1] = pre
        field = near[1][0][near[1][1], 256:512].astype(F32)
        mid = round_bf(field + pre * jax.nn.sigmoid(pre))
        ref, at = xm(a)
        put_stack(ref, at, masked(mid, a, pair, pairs))
    for a in range(-2, 6):
        near = [xm(a + p - 1) for p in range(3)]
        pre = conv_cell(mat, 1, [ref[at] for ref, at in near])
        pre1_ref[a + 2] = pre
        if 0 <= a < 4:
            mid = near[1][0][near[1][1], 256:512].astype(F32)
            top = (mid + pre * jax.nn.sigmoid(pre)).reshape(32, 8, 256).astype(BF)
            mine = even if a < 2 else jnp.logical_not(even)

            @pl.when(mine)
            def _():
                top_own[:, a % 2] = top

            @pl.when(jnp.logical_not(mine))
            def _():
                top_oth[:, a % 2] = top


SLAB = jax.ShapeDtypeStruct((32, 2, 8, 256), BF)
STACK = jax.ShapeDtypeStruct((6, 768, 256), BF)


def run_forward(pairs, pos, slabs, mats):
    return pl.pallas_call(
        functools.partial(forward_kernel, pairs),
        in_specs=[SM] + [VM] * 7,
        out_specs=[VM] * 6,
        out_shape=[
            STACK,
            STACK,
            jax.ShapeDtypeStruct((6, 256, 256), F32),
            jax.ShapeDtypeStruct((8, 256, 256), F32),
            SLAB,
            SLAB,
        ],
        scratch_shapes=[pltpu.VMEM((6, 768, 256), BF), pltpu.VMEM((4, 768, 256), BF)],
        compiler_params=pltpu.CompilerParams(vmem_limit_bytes=16 * MIB),
        name="forward",
    )(pos, *slabs, mats)


def kernel_grad(delta_ref, x_ref, scr, keep_ref, send_ref, kept):
    delta = jnp.concatenate([delta_ref(a) for a in range(4)], axis=1)
    for p in range(3):
        field = jnp.concatenate([x_ref[a + p] for a in range(4)], axis=1)
        full = lax.dot_general(
            delta, field, (((1,), (1,)), ((), ())), preferred_element_type=F32
        )
        for t in range(6):
            scr[6 * p + t] = full[:, 128 * t : 128 * t + 128]
    lane_row = lax.broadcasted_iota(jnp.int32, (256, 128), 0)
    fold_lane = lax.broadcasted_iota(jnp.int32, (256, 128), 1)
    total = None
    for d in range(8):
        rows = jnp.concatenate(
            [
                jnp.concatenate(
                    [scr[2 * n + t, pl.ds(d, 32, stride=8), :] for t in range(2)], axis=1
                )
                for n in range(9)
            ],
            axis=0,
        )
        high = rows.astype(BF)
        low = (rows - high.astype(F32)).astype(BF)
        fold = jnp.where(
            ((lane_row // 8) == (fold_lane % 32))
            & ((lane_row % 8) == d - 1 + fold_lane // 32)
            & (fold_lane < 96),
            1.0,
            0.0,
        ).astype(BF)
        term = jnp.dot(high, fold, preferred_element_type=F32) + jnp.dot(
            low, fold, preferred_element_type=F32
        )
        total = term if total is None else total + term

    ninth = total[256:288]
    free = lax.broadcasted_iota(jnp.int32, (32, 128), 1) >= 96
    groups = [
        jnp.where(free, pltpu.roll(ninth, 96 - 32 * q, 1), total[32 * q : 32 * q + 32])
        if q < 2
        else jnp.where(free, pltpu.roll(ninth, 32, 1), total[64:96])
        for q in range(3)
    ]
    total = jnp.concatenate(groups + [total[96:256]], axis=0)

    @pl.when(kept)
    def _():
        keep_ref[...] = total

    @pl.when(jnp.logical_not(kept))
    def _():
        send_ref[...] = total


def backward_kernel(pairs, pos_ref, own, partner, nc, ns, mat, xv_ref, xm_ref, pre0_ref,
                    pre1_ref, xd0_ref, bm_ref, keep_ref, send_ref, xd1_s, scr, cot_s):
    z = pos_ref[0]
    pair = pos_ref[1]
    even = z == 0
    zero_section = pos_ref[2] == 0
    slabs = [(nc, ns), (own, partner), (partner, own), (ns, nc)]
    for a in range(-2, 6):
        j = a + 2
        first, second = slabs[j // 2]
        cot = jnp.where(even, load_cell(first, j % 2), load_cell(second, j % 2))
        put_stack(xd1_s, j, round_bf(cot * slope(pre1_ref[j])))
        if -1 <= a < 5:
            cot_s[a + 1] = cot
    for a in range(-1, 5):
        pre = conv_cell(mat, 1, [xd1_s[a + 2 + p - 1] for p in range(3)])
        back = round_bf(cot_s[a + 1] + pre)
        if 0 <= a < 4:
            bm_ref[a] = back.astype(BF)
        delta = round_bf(back * slope(pre0_ref[a + 1]))
        put_stack(xd0_ref, a + 1, masked(delta, a, pair, pairs))

    kernel_grad(
        lambda a: xd0_ref[a + 1, 256:512], xv_ref, scr, keep_ref, send_ref, zero_section
    )
    kernel_grad(
        lambda a: xd1_s[a + 2, 256:512], xm_ref, scr, keep_ref, send_ref,
        jnp.logical_not(zero_section),
    )


def run_backward(pairs, pos, slabs, mats, xv, xm, pre0, pre1):
    grad = jax.ShapeDtypeStruct((256, 128), F32)
    return pl.pallas_call(
        functools.partial(backward_kernel, pairs),
        in_specs=[SM] + [VM] * 9,
        out_specs=[VM] * 4,
        out_shape=[STACK, jax.ShapeDtypeStruct((4, 256, 256), BF), grad, grad],
        scratch_shapes=[
            pltpu.VMEM((8, 768, 256), BF),
            pltpu.VMEM((18, 256, 128), F32),
            pltpu.VMEM((6, 256, 256), F32),
        ],
        compiler_params=pltpu.CompilerParams(vmem_limit_bytes=16 * MIB),
        name="backward",
    )(pos, *slabs, mats, xv, xm, pre0, pre1)


def last_kernel(pos_ref, xd0_ref, bm_ref, mat, out_own, out_oth):
    even = pos_ref[0] == 0
    for a in range(4):
        pre = conv_cell(mat, 0, [xd0_ref[a + p] for p in range(3)])
        out = (bm_ref[a].astype(F32) + pre).reshape(32, 8, 256).astype(BF)
        mine = even if a < 2 else jnp.logical_not(even)

        @pl.when(mine)
        def _():
            out_own[:, a % 2] = out

        @pl.when(jnp.logical_not(mine))
        def _():
            out_oth[:, a % 2] = out


def run_last(pos, xd0, bm, mats):
    return pl.pallas_call(
        last_kernel,
        in_specs=[SM] + [VM] * 3,
        out_specs=[VM] * 2,
        out_shape=[SLAB, SLAB],
        compiler_params=pltpu.CompilerParams(vmem_limit_bytes=6 * MIB),
        name="last",
    )(pos, xd0, bm, mats)


def gather_kernel(pos_ref, own0, own1, part, sec, both, out_ref, sems):
    z = pos_ref[0]
    s = pos_ref[2]

    def piece(n, ref):
        clip = 2 * (s ^ (n // 2)) + (z ^ (n % 2))
        return pltpu.make_async_copy(ref, out_ref.at[clip], sems.at[n])

    @pl.when(s == 0)
    def _():
        piece(0, own0).start()

    @pl.when(s == 1)
    def _():
        piece(0, own1).start()

    for n, ref in ((1, part), (2, sec), (3, both)):
        piece(n, ref).start()
    for n, ref in ((0, own0), (1, part), (2, sec), (3, both)):
        piece(n, ref).wait()


def run_gather(pos, pieces):
    return pl.pallas_call(
        gather_kernel,
        in_specs=[SM] + [VM] * 5,
        out_specs=pl.BlockSpec(memory_space=pl.ANY),
        out_shape=jax.ShapeDtypeStruct((4, 32, 2, 8, 256), BF),
        scratch_shapes=[pltpu.SemaphoreType.DMA((4,))],
        compiler_params=pltpu.CompilerParams(vmem_limit_bytes=2 * MIB),
        name="gather",
    )(pos, *pieces)


def unfold_kernel(a_ref, b_ref, c_ref, d_ref, out_ref):
    for n in range(8):
        rows = slice(32 * n, 32 * n + 32)
        value = (a_ref[rows] + b_ref[rows]) + (c_ref[rows] + d_ref[rows])
        p, r = divmod(n, 3)
        for q in range(3):
            out_ref[(p * 3 + q) * 3 + r] = value[:, 32 * q : 32 * q + 32]
        if n < 3:
            out_ref[(6 + n) * 3 + 2] = value[:, 96:128]


def run_unfold(parts):
    return pl.pallas_call(
        unfold_kernel,
        out_shape=jax.ShapeDtypeStruct((27, 32, 32), F32),
        compiler_params=pltpu.CompilerParams(vmem_limit_bytes=4 * MIB),
        name="unfold",
    )(*parts)


def body(volume, cotangent, weights):
    s = lax.axis_index("section")
    l = lax.axis_index("lat")
    pairs = lax.axis_size("lat") // 2
    z = l % 2
    pos = jnp.stack([z, l // 2, s]).astype(jnp.int32)

    def clip(array, at):
        return lax.dynamic_index_in_dim(array, at, 0, keepdims=False)

    same = 2 * s + z
    cross = 2 * s + (1 - z)
    straight = jnp.transpose(weights[0], (2, 3, 4, 0, 1)).reshape(27, 32, 32)
    mine = jnp.stack([straight, jnp.swapaxes(straight, 1, 2)])
    others = permute(mine, other_section)
    v_same, v_cross = clip(volume, same), clip(volume, cross)
    slabs = [
        v_same,
        permute(v_cross, PARTNER),
        permute(v_cross, NEAR_CROSS),
        permute(v_same, NEAR_SAME),
        permute(v_cross, FAR_CROSS),
        permute(v_same, FAR_SAME),
    ]
    c_same, c_cross = clip(cotangent, same), clip(cotangent, cross)
    c_slabs = [
        c_same,
        permute(c_cross, PARTNER),
        permute(c_cross, NEAR_CROSS),
        permute(c_same, NEAR_SAME),
    ]
    fwd, bwd = make_bands(pos, mine, others)
    xv, xm, pre0, pre1, top_own, top_oth = run_forward(pairs, pos, slabs, fwd)
    xd0, bm, keep, send = run_backward(pairs, pos, c_slabs, bwd, xv, xm, pre0, pre1)
    total = keep + permute(send, other_section)
    bm, total = lax.optimization_barrier((bm, total))
    out_own, out_oth = run_last(pos, xd0, bm, bwd)
    for axis in (2, 1, 0):
        parts = [total] + [permute(total, ring(axis, step)) for step in (2, 1, 3)]
        if axis:
            total = (parts[0] + parts[1]) + (parts[2] + parts[3])
    at_zero = s == 0
    pieces = [
        out_own,
        top_own,
        permute(jnp.where(at_zero, out_oth, top_oth), PARTNER),
        permute(jnp.where(at_zero, top_own, out_own), other_section),
        permute(jnp.where(at_zero, top_oth, out_oth), other_both),
    ]
    field = run_gather(pos, pieces)
    grads = run_unfold(parts).reshape(3, 3, 3, 32, 32)
    return (field[None], jnp.transpose(grads, (3, 4, 0, 1, 2))[None])


def solution(mesh):
    return jax.shard_map(
        body,
        mesh=mesh,
        in_specs=(
            P("dp", None, "lat", None, None),
            P("dp", None, "lat", None, None),
            P("section", None, None, None, None, None),
        ),
        out_specs=(
            P("section", "dp", None, "lat", None, None),
            P("section", None, None, None, None, None),
        ),
        check_vma=False,
    )
```

```python
import functools

import jax
import jax.numpy as jnp
from jax import lax
from jax.experimental import pallas as pl
from jax.experimental.pallas import tpu as pltpu
from jax.sharding import PartitionSpec as P

AXES = ("section", "lat", "dp")
BF = jnp.bfloat16
F32 = jnp.float32
MIB = 1024 * 1024
VM = pl.BlockSpec(memory_space=pltpu.MemorySpace.VMEM)
SM = pl.BlockSpec(memory_space=pltpu.MemorySpace.SMEM)


def permute(value, move):
    sizes = [lax.axis_size(a) for a in AXES]
    pairs = []
    for s in range(sizes[0]):
        for l in range(sizes[1]):
            for d in range(sizes[2]):
                target = move(s, l, d)
                if target is None or not 0 <= target[1] < sizes[1]:
                    continue
                source_id = (s * sizes[1] + l) * sizes[2] + d
                target_id = (target[0] * sizes[1] + target[1]) * sizes[2] + target[2]
                pairs.append((source_id, target_id))
    return lax.ppermute(value, AXES, pairs)


def lat_move(even, odd):
    return lambda s, l, d: (s, l + (odd if l % 2 else even), d)


PARTNER = lat_move(1, -1)
NEAR_CROSS = lat_move(-1, 1)
NEAR_SAME = lat_move(-2, 2)
FAR_SAME = lat_move(2, -2)
FAR_CROSS = lat_move(3, -3)


def other_section(s, l, d):
    return (1 - s, l, d)


def ring(axis, step):
    def move(s, l, d):
        at = [l // 8, (l // 2) % 4, d * 2 + l % 2]
        at[axis] = (at[axis] + step) % 4
        return (s, at[0] * 8 + at[1] * 2 + at[2] % 2, at[2] // 2)

    return move


def other_both(s, l, d):
    return (1 - s, l ^ 1, d)


def load_cell(ref, plane, cell):
    part = ref[:, cell] if len(ref.shape) == 4 else ref[plane, :, cell]
    return part.astype(F32).reshape(256, 256)


def put_stack(ref, at, value):
    lane = lax.broadcasted_iota(jnp.int32, (256, 256), 1)
    before = jnp.where(lane == 0, 0.0, pltpu.roll(value, 1, 1))
    after = jnp.where(lane == 255, 0.0, pltpu.roll(value, 255, 1))
    ref[at, 0:256] = before.astype(BF)
    ref[at, 256:512] = value.astype(BF)
    ref[at, 512:768] = after.astype(BF)


def conv_cell(mat, block, slices):
    total = None
    for p in range(3):
        term = jnp.dot(mat[block, p], slices[p], preferred_element_type=F32)
        total = term if total is None else total + term
    return total


def round_bf(value):
    return value.astype(BF).astype(F32)


def slope(value):
    sig = jax.nn.sigmoid(value)
    return sig * (1.0 + value * (1.0 - sig))


def band_kernel(pos_ref, mine_ref, others_ref, fwd_ref, bwd_ref):
    row = lax.broadcasted_iota(jnp.int32, (256, 256), 0) % 8
    lane = lax.broadcasted_iota(jnp.int32, (256, 256), 1) % 8
    gap = lane - row
    spread = jnp.where(
        lax.broadcasted_iota(jnp.int32, (32, 256), 1) // 8
        == lax.broadcasted_iota(jnp.int32, (32, 256), 0),
        1.0,
        0.0,
    ).astype(BF)
    tall = jnp.where(
        lax.broadcasted_iota(jnp.int32, (256, 32), 0) // 8
        == lax.broadcasted_iota(jnp.int32, (256, 32), 1),
        1.0,
        0.0,
    ).astype(BF)
    for src, block in ((mine_ref, pos_ref[2]), (others_ref, 1 - pos_ref[2])):
        for back in range(2):
            out_ref = bwd_ref if back else fwd_ref
            wide = jnp.dot(
                src[back].reshape(864, 32), spread, preferred_element_type=F32
            ).astype(BF)
            for p in range(3):
                for r in range(3):
                    mat = jnp.zeros((256, 256), F32)
                    for q in range(3):
                        n = (p * 3 + q) * 3 + r
                        if back:
                            n = 26 - n
                        full = jnp.dot(
                            tall, wide[32 * n : 32 * n + 32], preferred_element_type=F32
                        )
                        mat = jnp.where(gap == q - 1, full, mat)
                    out_ref[block, p, :, 256 * r : 256 * r + 256] = mat.astype(BF)


def make_bands(pos, mine, others):
    return pl.pallas_call(
        band_kernel,
        in_specs=[SM, VM, VM],
        out_specs=[VM, VM],
        out_shape=[jax.ShapeDtypeStruct((2, 3, 256, 768), BF)] * 2,
        compiler_params=pltpu.CompilerParams(vmem_limit_bytes=8 * MIB),
        name="bands",
    )(pos, mine, others)


def valid_cell(at, pair, pairs):
    if at < 0:
        return pair > 0
    if at >= 4:
        return pair < pairs - 1
    return None


def masked(value, at, pair, pairs):
    ok = valid_cell(at, pair, pairs)
    return value if ok is None else jnp.where(ok, value, 0.0)


def pick_slab(refs, z):
    own, partner, nc, ns, fc, fs = refs
    return [(fs, fc), (nc, ns), (own, partner), (partner, own), (ns, nc), (fc, fs)]


def forward_kernel(pairs, pos_ref, own, partner, nc, ns, fc, fs, mat,
                   xv_ref, xm_ref, pre0_ref, pre1_ref, top_own, top_oth, xv_s, xm_s):
    z = pos_ref[0]
    pair = pos_ref[1]
    even = z == 0
    slabs = pick_slab((own, partner, nc, ns, fc, fs), z)

    def xv(a):
        return (xv_ref, a + 1) if -1 <= a < 5 else (xv_s, a + 4 if a < -1 else a - 2)

    def xm(a):
        return (xm_ref, a + 1) if -1 <= a < 5 else (xm_s, a + 3 if a < -1 else a - 3)

    for a in range(-4, 8):
        j = a + 4
        first, second = slabs[j // 2]
        value = jnp.where(even, load_cell(first, 0, j % 2), load_cell(second, 0, j % 2))
        ref, at = xv(a)
        put_stack(ref, at, value)
    for a in range(-3, 7):
        near = [xv(a + p - 1) for p in range(3)]
        pre = conv_cell(mat, 0, [ref[at] for ref, at in near])
        if -1 <= a < 5:
            pre0_ref[a + 1] = pre
        field = near[1][0][near[1][1], 256:512].astype(F32)
        mid = round_bf(field + pre * jax.nn.sigmoid(pre))
        ref, at = xm(a)
        put_stack(ref, at, masked(mid, a, pair, pairs))
    for a in range(-2, 6):
        near = [xm(a + p - 1) for p in range(3)]
        pre = conv_cell(mat, 1, [ref[at] for ref, at in near])
        pre1_ref[a + 2] = pre
        if 0 <= a < 4:
            mid = near[1][0][near[1][1], 256:512].astype(F32)
            top = (mid + pre * jax.nn.sigmoid(pre)).reshape(32, 8, 256).astype(BF)
            mine = even if a < 2 else jnp.logical_not(even)

            @pl.when(mine)
            def _():
                top_own[:, a % 2] = top

            @pl.when(jnp.logical_not(mine))
            def _():
                top_oth[:, a % 2] = top


SLAB = jax.ShapeDtypeStruct((32, 2, 8, 256), BF)
STACK = jax.ShapeDtypeStruct((6, 768, 256), BF)


def run_forward(pairs, pos, slabs, mats):
    return pl.pallas_call(
        functools.partial(forward_kernel, pairs),
        in_specs=[SM] + [VM] * 7,
        out_specs=[VM] * 6,
        out_shape=[
            STACK,
            STACK,
            jax.ShapeDtypeStruct((6, 256, 256), F32),
            jax.ShapeDtypeStruct((8, 256, 256), F32),
            SLAB,
            SLAB,
        ],
        scratch_shapes=[pltpu.VMEM((6, 768, 256), BF), pltpu.VMEM((4, 768, 256), BF)],
        compiler_params=pltpu.CompilerParams(vmem_limit_bytes=16 * MIB),
        name="forward",
    )(pos, *slabs, mats)


def kernel_grad(delta_ref, x_ref, scr, keep_ref, send_ref, kept):
    delta = jnp.concatenate([delta_ref(a) for a in range(4)], axis=1)
    for p in range(3):
        field = jnp.concatenate([x_ref[a + p] for a in range(4)], axis=1)
        full = lax.dot_general(
            delta, field, (((1,), (1,)), ((), ())), preferred_element_type=F32
        )
        for t in range(6):
            scr[6 * p + t] = full[:, 128 * t : 128 * t + 128]
    lane_row = lax.broadcasted_iota(jnp.int32, (256, 128), 0)
    fold_lane = lax.broadcasted_iota(jnp.int32, (256, 128), 1)
    total = None
    for d in range(8):
        rows = jnp.concatenate(
            [
                jnp.concatenate(
                    [scr[2 * n + t, pl.ds(d, 32, stride=8), :] for t in range(2)], axis=1
                )
                for n in range(9)
            ],
            axis=0,
        )
        high = rows.astype(BF)
        low = (rows - high.astype(F32)).astype(BF)
        fold = jnp.where(
            ((lane_row // 8) == (fold_lane % 32))
            & ((lane_row % 8) == d - 1 + fold_lane // 32)
            & (fold_lane < 96),
            1.0,
            0.0,
        ).astype(BF)
        term = jnp.dot(high, fold, preferred_element_type=F32) + jnp.dot(
            low, fold, preferred_element_type=F32
        )
        total = term if total is None else total + term

    ninth = total[256:288]
    free = lax.broadcasted_iota(jnp.int32, (32, 128), 1) >= 96
    groups = [
        jnp.where(free, pltpu.roll(ninth, 96 - 32 * q, 1), total[32 * q : 32 * q + 32])
        if q < 2
        else jnp.where(free, pltpu.roll(ninth, 32, 1), total[64:96])
        for q in range(3)
    ]
    total = jnp.concatenate(groups + [total[96:256]], axis=0)

    @pl.when(kept)
    def _():
        keep_ref[...] = total

    @pl.when(jnp.logical_not(kept))
    def _():
        send_ref[...] = total


def backward_kernel(pairs, pos_ref, own, partner, nc, ns, mat, xv_ref, xm_ref, pre0_ref,
                    pre1_ref, d0_ref, bm_ref, keep_ref, send_ref, xd1_s, scr, cot_s):
    z = pos_ref[0]
    pair = pos_ref[1]
    even = z == 0
    zero_section = pos_ref[2] == 0
    slabs = [(nc, ns), (own, partner), (partner, own), (ns, nc)]
    for a in range(-2, 6):
        j = a + 2
        first, second = slabs[j // 2]
        cot = jnp.where(even, load_cell(first, 1, j % 2), load_cell(second, 1, j % 2))
        put_stack(xd1_s, j, round_bf(cot * slope(pre1_ref[j])))
        if -1 <= a < 5:
            cot_s[a + 1] = cot
    for a in range(-1, 5):
        pre = conv_cell(mat, 1, [xd1_s[a + 2 + p - 1] for p in range(3)])
        back = round_bf(cot_s[a + 1] + pre)
        if 0 <= a < 4:
            bm_ref[a] = back.astype(BF)
        delta = round_bf(back * slope(pre0_ref[a + 1]))
        d0_ref[a + 1] = masked(delta, a, pair, pairs).astype(BF)

    kernel_grad(
        lambda a: d0_ref[a + 1], xv_ref, scr, keep_ref, send_ref, zero_section
    )
    kernel_grad(
        lambda a: xd1_s[a + 2, 256:512], xm_ref, scr, keep_ref, send_ref,
        jnp.logical_not(zero_section),
    )


def run_backward(pairs, pos, slabs, mats, xv, xm, pre0, pre1):
    grad = jax.ShapeDtypeStruct((256, 128), F32)
    return pl.pallas_call(
        functools.partial(backward_kernel, pairs),
        in_specs=[SM] + [VM] * 9,
        out_specs=[VM] * 4,
        out_shape=[
            jax.ShapeDtypeStruct((6, 256, 256), BF),
            jax.ShapeDtypeStruct((4, 256, 256), BF),
            grad,
            grad,
        ],
        scratch_shapes=[
            pltpu.VMEM((8, 768, 256), BF),
            pltpu.VMEM((18, 256, 128), F32),
            pltpu.VMEM((6, 256, 256), F32),
        ],
        compiler_params=pltpu.CompilerParams(vmem_limit_bytes=16 * MIB),
        name="backward",
    )(pos, *slabs, mats, xv, xm, pre0, pre1)


def last_kernel(pos_ref, d0_ref, bm_ref, mat, out_own, out_oth, xd0_ref):
    even = pos_ref[0] == 0
    for a in range(6):
        put_stack(xd0_ref, a, d0_ref[a].astype(F32))
    for a in range(4):
        pre = conv_cell(mat, 0, [xd0_ref[a + p] for p in range(3)])
        out = (bm_ref[a].astype(F32) + pre).reshape(32, 8, 256).astype(BF)
        mine = even if a < 2 else jnp.logical_not(even)

        @pl.when(mine)
        def _():
            out_own[:, a % 2] = out

        @pl.when(jnp.logical_not(mine))
        def _():
            out_oth[:, a % 2] = out


def run_last(pos, xd0, bm, mats):
    return pl.pallas_call(
        last_kernel,
        in_specs=[SM] + [VM] * 3,
        out_specs=[VM] * 2,
        out_shape=[SLAB, SLAB],
        scratch_shapes=[pltpu.VMEM((6, 768, 256), BF)],
        compiler_params=pltpu.CompilerParams(vmem_limit_bytes=10 * MIB),
        name="last",
    )(pos, xd0, bm, mats)


def gather_kernel(pos_ref, own0, own1, part, sec, both, out_ref, sems):
    z = pos_ref[0]
    s = pos_ref[2]

    def piece(n, ref):
        clip = 2 * (s ^ (n // 2)) + (z ^ (n % 2))
        return pltpu.make_async_copy(ref, out_ref.at[clip], sems.at[n])

    @pl.when(s == 0)
    def _():
        piece(0, own0).start()

    @pl.when(s == 1)
    def _():
        piece(0, own1).start()

    for n, ref in ((1, part), (2, sec), (3, both)):
        piece(n, ref).start()
    for n, ref in ((0, own0), (1, part), (2, sec), (3, both)):
        piece(n, ref).wait()


def run_gather(pos, pieces):
    return pl.pallas_call(
        gather_kernel,
        in_specs=[SM] + [VM] * 5,
        out_specs=pl.BlockSpec(memory_space=pl.ANY),
        out_shape=jax.ShapeDtypeStruct((4, 32, 2, 8, 256), BF),
        scratch_shapes=[pltpu.SemaphoreType.DMA((4,))],
        compiler_params=pltpu.CompilerParams(vmem_limit_bytes=2 * MIB),
        name="gather",
    )(pos, *pieces)


def unfold_kernel(a_ref, b_ref, c_ref, d_ref, out_ref):
    for n in range(8):
        rows = slice(32 * n, 32 * n + 32)
        value = (a_ref[rows] + b_ref[rows]) + (c_ref[rows] + d_ref[rows])
        p, r = divmod(n, 3)
        for q in range(3):
            out_ref[(p * 3 + q) * 3 + r] = value[:, 32 * q : 32 * q + 32]
        if n < 3:
            out_ref[(6 + n) * 3 + 2] = value[:, 96:128]


def run_unfold(parts):
    return pl.pallas_call(
        unfold_kernel,
        out_shape=jax.ShapeDtypeStruct((27, 32, 32), F32),
        compiler_params=pltpu.CompilerParams(vmem_limit_bytes=4 * MIB),
        name="unfold",
    )(*parts)


def body(volume, cotangent, weights):
    s = lax.axis_index("section")
    l = lax.axis_index("lat")
    pairs = lax.axis_size("lat") // 2
    z = l % 2
    pos = jnp.stack([z, l // 2, s]).astype(jnp.int32)

    def clip(array, at):
        return lax.dynamic_index_in_dim(array, at, 0, keepdims=False)

    same = 2 * s + z
    cross = 2 * s + (1 - z)
    straight = jnp.transpose(weights[0], (2, 3, 4, 0, 1)).reshape(27, 32, 32)
    mine = jnp.stack([straight, jnp.swapaxes(straight, 1, 2)])
    others = permute(mine, other_section)
    v_same, v_cross = clip(volume, same), clip(volume, cross)
    c_same, c_cross = clip(cotangent, same), clip(cotangent, cross)
    near_same = permute(jnp.stack([v_same, c_same]), NEAR_SAME)
    slabs = [
        v_same,
        permute(v_cross, PARTNER),
        permute(v_cross, NEAR_CROSS),
        near_same,
        permute(v_cross, FAR_CROSS),
        permute(v_same, FAR_SAME),
    ]
    c_slabs = [
        c_same,
        permute(c_cross, PARTNER),
        permute(c_cross, NEAR_CROSS),
        near_same,
    ]
    fwd, bwd = make_bands(pos, mine, others)
    xv, xm, pre0, pre1, top_own, top_oth = run_forward(pairs, pos, slabs, fwd)
    xd0, bm, keep, send = run_backward(pairs, pos, c_slabs, bwd, xv, xm, pre0, pre1)
    total = keep + permute(send, other_section)
    bm, total = lax.optimization_barrier((bm, total))
    out_own, out_oth = run_last(pos, xd0, bm, bwd)
    for axis in (2, 1, 0):
        parts = [total] + [permute(total, ring(axis, step)) for step in (2, 1, 3)]
        if axis:
            total = (parts[0] + parts[1]) + (parts[2] + parts[3])
    at_zero = s == 0
    pieces = [
        out_own,
        top_own,
        permute(jnp.where(at_zero, out_oth, top_oth), PARTNER),
        permute(jnp.where(at_zero, top_own, out_own), other_section),
        permute(jnp.where(at_zero, top_oth, out_oth), other_both),
    ]
    field = run_gather(pos, pieces)
    grads = run_unfold(parts).reshape(3, 3, 3, 32, 32)
    return (field[None], jnp.transpose(grads, (3, 4, 0, 1, 2))[None])


def solution(mesh):
    return jax.shard_map(
        body,
        mesh=mesh,
        in_specs=(
            P("dp", None, "lat", None, None),
            P("dp", None, "lat", None, None),
            P("section", None, None, None, None, None),
        ),
        out_specs=(
            P("section", "dp", None, "lat", None, None),
            P("section", None, None, None, None, None),
        ),
        check_vma=False,
    )
```

```python
import functools

import jax
import jax.numpy as jnp
from jax import lax
from jax.experimental import pallas as pl
from jax.experimental.pallas import tpu as pltpu
from jax.sharding import PartitionSpec as P

AXES = ("section", "lat", "dp")
BF = jnp.bfloat16
F32 = jnp.float32
MIB = 1024 * 1024
VM = pl.BlockSpec(memory_space=pltpu.MemorySpace.VMEM)
SM = pl.BlockSpec(memory_space=pltpu.MemorySpace.SMEM)


def permute(value, move):
    sizes = [lax.axis_size(a) for a in AXES]
    pairs = []
    for s in range(sizes[0]):
        for l in range(sizes[1]):
            for d in range(sizes[2]):
                target = move(s, l, d)
                if target is None or not 0 <= target[1] < sizes[1]:
                    continue
                source_id = (s * sizes[1] + l) * sizes[2] + d
                target_id = (target[0] * sizes[1] + target[1]) * sizes[2] + target[2]
                pairs.append((source_id, target_id))
    return lax.ppermute(value, AXES, pairs)


def lat_move(even, odd):
    return lambda s, l, d: (s, l + (odd if l % 2 else even), d)


PARTNER = lat_move(1, -1)
NEAR_CROSS = lat_move(-1, 1)
NEAR_SAME = lat_move(-2, 2)
FAR_SAME = lat_move(2, -2)
FAR_CROSS = lat_move(3, -3)


def other_section(s, l, d):
    return (1 - s, l, d)


def ring(axis, step):
    def move(s, l, d):
        at = [l // 8, (l // 2) % 4, d * 2 + l % 2]
        at[axis] = (at[axis] + step) % 4
        return (s, at[0] * 8 + at[1] * 2 + at[2] % 2, at[2] // 2)

    return move


def other_both(s, l, d):
    return (1 - s, l ^ 1, d)


def load_cell(ref, plane, cell):
    part = ref[:, cell] if len(ref.shape) == 4 else ref[plane, :, cell]
    return part.astype(F32).reshape(256, 256)


def put_stack(ref, at, value):
    lane = lax.broadcasted_iota(jnp.int32, (256, 256), 1)
    before = jnp.where(lane == 0, 0.0, pltpu.roll(value, 1, 1))
    after = jnp.where(lane == 255, 0.0, pltpu.roll(value, 255, 1))
    ref[at, 0:256] = before.astype(BF)
    ref[at, 256:512] = value.astype(BF)
    ref[at, 512:768] = after.astype(BF)


def conv_cell(mat, block, slices):
    total = None
    for p in range(3):
        term = jnp.dot(mat[block, p], slices[p], preferred_element_type=F32)
        total = term if total is None else total + term
    return total


def round_bf(value):
    return value.astype(BF).astype(F32)


def slope(value):
    sig = jax.nn.sigmoid(value)
    return sig * (1.0 + value * (1.0 - sig))


def band_kernel(pos_ref, mine_ref, others_ref, fwd_ref, bwd_ref):
    row = lax.broadcasted_iota(jnp.int32, (256, 256), 0) % 8
    lane = lax.broadcasted_iota(jnp.int32, (256, 256), 1) % 8
    gap = lane - row
    spread = jnp.where(
        lax.broadcasted_iota(jnp.int32, (32, 256), 1) // 8
        == lax.broadcasted_iota(jnp.int32, (32, 256), 0),
        1.0,
        0.0,
    ).astype(BF)
    tall = jnp.where(
        lax.broadcasted_iota(jnp.int32, (256, 32), 0) // 8
        == lax.broadcasted_iota(jnp.int32, (256, 32), 1),
        1.0,
        0.0,
    ).astype(BF)
    for src, block in ((mine_ref, pos_ref[2]), (others_ref, 1 - pos_ref[2])):
        for back in range(2):
            out_ref = bwd_ref if back else fwd_ref
            wide = jnp.dot(
                src[back].reshape(864, 32), spread, preferred_element_type=F32
            ).astype(BF)
            for p in range(3):
                for r in range(3):
                    mat = jnp.zeros((256, 256), F32)
                    for q in range(3):
                        n = (p * 3 + q) * 3 + r
                        if back:
                            n = 26 - n
                        full = jnp.dot(
                            tall, wide[32 * n : 32 * n + 32], preferred_element_type=F32
                        )
                        mat = jnp.where(gap == q - 1, full, mat)
                    out_ref[block, p, :, 256 * r : 256 * r + 256] = mat.astype(BF)


def make_bands(pos, mine, others):
    return pl.pallas_call(
        band_kernel,
        in_specs=[SM, VM, VM],
        out_specs=[VM, VM],
        out_shape=[jax.ShapeDtypeStruct((2, 3, 256, 768), BF)] * 2,
        compiler_params=pltpu.CompilerParams(vmem_limit_bytes=8 * MIB),
        name="bands",
    )(pos, mine, others)


def valid_cell(at, pair, pairs):
    if at < 0:
        return pair > 0
    if at >= 4:
        return pair < pairs - 1
    return None


def masked(value, at, pair, pairs):
    ok = valid_cell(at, pair, pairs)
    return value if ok is None else jnp.where(ok, value, 0.0)


def pick_slab(refs, z):
    own, partner, nc, ns, fc, fs = refs
    return [(fs, fc), (nc, ns), (own, partner), (partner, own), (ns, nc), (fc, fs)]


def forward_kernel(pairs, pos_ref, own, partner, nc, ns, fc, fs, mat,
                   xv_ref, xm_ref, pre0_ref, pre1_ref, top_own, top_oth, xv_s, xm_s):
    z = pos_ref[0]
    pair = pos_ref[1]
    even = z == 0
    slabs = pick_slab((own, partner, nc, ns, fc, fs), z)

    def xv(a):
        return (xv_ref, a + 1) if -1 <= a < 5 else (xv_s, a + 4 if a < -1 else a - 2)

    def xm(a):
        return (xm_ref, a + 1) if -1 <= a < 5 else (xm_s, a + 3 if a < -1 else a - 3)

    for a in range(-4, 8):
        j = a + 4
        first, second = slabs[j // 2]
        value = jnp.where(even, load_cell(first, 0, j % 2), load_cell(second, 0, j % 2))
        ref, at = xv(a)
        put_stack(ref, at, value)
    for a in range(-3, 7):
        near = [xv(a + p - 1) for p in range(3)]
        pre = conv_cell(mat, 0, [ref[at] for ref, at in near])
        if -1 <= a < 5:
            pre0_ref[a + 1] = pre
        field = near[1][0][near[1][1], 256:512].astype(F32)
        mid = round_bf(field + pre * jax.nn.sigmoid(pre))
        ref, at = xm(a)
        put_stack(ref, at, masked(mid, a, pair, pairs))
    for a in range(-2, 6):
        near = [xm(a + p - 1) for p in range(3)]
        pre = conv_cell(mat, 1, [ref[at] for ref, at in near])
        pre1_ref[a + 2] = pre
        if 0 <= a < 4:
            mid = near[1][0][near[1][1], 256:512].astype(F32)
            top = (mid + pre * jax.nn.sigmoid(pre)).reshape(32, 8, 256).astype(BF)
            mine = even if a < 2 else jnp.logical_not(even)

            @pl.when(mine)
            def _():
                top_own[:, a % 2] = top

            @pl.when(jnp.logical_not(mine))
            def _():
                top_oth[:, a % 2] = top


SLAB = jax.ShapeDtypeStruct((32, 2, 8, 256), BF)
STACK = jax.ShapeDtypeStruct((6, 768, 256), BF)


def run_forward(pairs, pos, slabs, mats):
    return pl.pallas_call(
        functools.partial(forward_kernel, pairs),
        in_specs=[SM] + [VM] * 7,
        out_specs=[VM] * 6,
        out_shape=[
            STACK,
            STACK,
            jax.ShapeDtypeStruct((6, 256, 256), F32),
            jax.ShapeDtypeStruct((8, 256, 256), F32),
            SLAB,
            SLAB,
        ],
        scratch_shapes=[pltpu.VMEM((6, 768, 256), BF), pltpu.VMEM((4, 768, 256), BF)],
        compiler_params=pltpu.CompilerParams(vmem_limit_bytes=16 * MIB),
        name="forward",
    )(pos, *slabs, mats)


def kernel_grad(delta_ref, x_ref, scr, keep_ref, send_ref, kept):
    delta = jnp.concatenate([delta_ref(a) for a in range(4)], axis=1)
    for p in range(3):
        field = jnp.concatenate([x_ref[a + p] for a in range(4)], axis=1)
        full = lax.dot_general(
            delta, field, (((1,), (1,)), ((), ())), preferred_element_type=F32
        )
        for t in range(6):
            scr[6 * p + t] = full[:, 128 * t : 128 * t + 128]
    lane_row = lax.broadcasted_iota(jnp.int32, (256, 128), 0)
    fold_lane = lax.broadcasted_iota(jnp.int32, (256, 128), 1)
    total = None
    for d in range(8):
        rows = jnp.concatenate(
            [
                jnp.concatenate(
                    [scr[2 * n + t, pl.ds(d, 32, stride=8), :] for t in range(2)], axis=1
                )
                for n in range(9)
            ],
            axis=0,
        )
        high = rows.astype(BF)
        low = (rows - high.astype(F32)).astype(BF)
        fold = jnp.where(
            ((lane_row // 8) == (fold_lane % 32))
            & ((lane_row % 8) == d - 1 + fold_lane // 32)
            & (fold_lane < 96),
            1.0,
            0.0,
        ).astype(BF)
        term = jnp.dot(high, fold, preferred_element_type=F32) + jnp.dot(
            low, fold, preferred_element_type=F32
        )
        total = term if total is None else total + term

    ninth = total[256:288]
    free = lax.broadcasted_iota(jnp.int32, (32, 128), 1) >= 96
    groups = [
        jnp.where(free, pltpu.roll(ninth, 96 - 32 * q, 1), total[32 * q : 32 * q + 32])
        if q < 2
        else jnp.where(free, pltpu.roll(ninth, 32, 1), total[64:96])
        for q in range(3)
    ]
    total = jnp.concatenate(groups + [total[96:256]], axis=0)

    @pl.when(kept)
    def _():
        keep_ref[...] = total

    @pl.when(jnp.logical_not(kept))
    def _():
        send_ref[...] = total


def backward_kernel(pairs, pos_ref, own, partner, nc, ns, mat, xv_ref, xm_ref, pre0_ref,
                    pre1_ref, d0_ref, keep_ref, send_ref, xd1_s, scr, cot_s):
    z = pos_ref[0]
    pair = pos_ref[1]
    even = z == 0
    zero_section = pos_ref[2] == 0
    slabs = [(nc, ns), (own, partner), (partner, own), (ns, nc)]
    for a in range(-2, 6):
        j = a + 2
        first, second = slabs[j // 2]
        cot = jnp.where(even, load_cell(first, 1, j % 2), load_cell(second, 1, j % 2))
        put_stack(xd1_s, j, round_bf(cot * slope(pre1_ref[j])))
        if -1 <= a < 5:
            cot_s[a + 1] = cot
    for a in range(-1, 5):
        pre = conv_cell(mat, 1, [xd1_s[a + 2 + p - 1] for p in range(3)])
        back = round_bf(cot_s[a + 1] + pre)
        if 0 <= a < 4:
            d0_ref[6 + a] = back.astype(BF)
        delta = round_bf(back * slope(pre0_ref[a + 1]))
        d0_ref[a + 1] = masked(delta, a, pair, pairs).astype(BF)

    kernel_grad(
        lambda a: d0_ref[a + 1], xv_ref, scr, keep_ref, send_ref, zero_section
    )
    kernel_grad(
        lambda a: xd1_s[a + 2, 256:512], xm_ref, scr, keep_ref, send_ref,
        jnp.logical_not(zero_section),
    )


def run_backward(pairs, pos, slabs, mats, xv, xm, pre0, pre1):
    grad = jax.ShapeDtypeStruct((256, 128), F32)
    return pl.pallas_call(
        functools.partial(backward_kernel, pairs),
        in_specs=[SM] + [VM] * 9,
        out_specs=[VM] * 3,
        out_shape=[
            jax.ShapeDtypeStruct((10, 256, 256), BF),
            grad,
            grad,
        ],
        scratch_shapes=[
            pltpu.VMEM((8, 768, 256), BF),
            pltpu.VMEM((18, 256, 128), F32),
            pltpu.VMEM((6, 256, 256), F32),
        ],
        compiler_params=pltpu.CompilerParams(vmem_limit_bytes=16 * MIB),
        name="backward",
    )(pos, *slabs, mats, xv, xm, pre0, pre1)


def last_kernel(pos_ref, d0_ref, mat, out_own, out_oth, xd0_ref):
    even = pos_ref[0] == 0
    for a in range(6):
        put_stack(xd0_ref, a, d0_ref[a].astype(F32))
    for a in range(4):
        pre = conv_cell(mat, 0, [xd0_ref[a + p] for p in range(3)])
        out = (d0_ref[6 + a].astype(F32) + pre).reshape(32, 8, 256).astype(BF)
        mine = even if a < 2 else jnp.logical_not(even)

        @pl.when(mine)
        def _():
            out_own[:, a % 2] = out

        @pl.when(jnp.logical_not(mine))
        def _():
            out_oth[:, a % 2] = out


def run_last(pos, d0, mats):
    return pl.pallas_call(
        last_kernel,
        in_specs=[SM] + [VM] * 2,
        out_specs=[VM] * 2,
        out_shape=[SLAB, SLAB],
        scratch_shapes=[pltpu.VMEM((6, 768, 256), BF)],
        compiler_params=pltpu.CompilerParams(vmem_limit_bytes=10 * MIB),
        name="last",
    )(pos, d0, mats)


def gather_kernel(pos_ref, own0, own1, part, sec, both, out_ref, sems):
    z = pos_ref[0]
    s = pos_ref[2]

    def piece(n, ref):
        clip = 2 * (s ^ (n // 2)) + (z ^ (n % 2))
        return pltpu.make_async_copy(ref, out_ref.at[clip], sems.at[n])

    @pl.when(s == 0)
    def _():
        piece(0, own0).start()

    @pl.when(s == 1)
    def _():
        piece(0, own1).start()

    for n, ref in ((1, part), (2, sec), (3, both)):
        piece(n, ref).start()
    for n, ref in ((0, own0), (1, part), (2, sec), (3, both)):
        piece(n, ref).wait()


def run_gather(pos, pieces):
    return pl.pallas_call(
        gather_kernel,
        in_specs=[SM] + [VM] * 5,
        out_specs=pl.BlockSpec(memory_space=pl.ANY),
        out_shape=jax.ShapeDtypeStruct((4, 32, 2, 8, 256), BF),
        scratch_shapes=[pltpu.SemaphoreType.DMA((4,))],
        compiler_params=pltpu.CompilerParams(vmem_limit_bytes=2 * MIB),
        name="gather",
    )(pos, *pieces)


def unfold_kernel(a_ref, b_ref, c_ref, d_ref, out_ref):
    for n in range(8):
        rows = slice(32 * n, 32 * n + 32)
        value = (a_ref[rows] + b_ref[rows]) + (c_ref[rows] + d_ref[rows])
        p, r = divmod(n, 3)
        for q in range(3):
            out_ref[(p * 3 + q) * 3 + r] = value[:, 32 * q : 32 * q + 32]
        if n < 3:
            out_ref[(6 + n) * 3 + 2] = value[:, 96:128]


def run_unfold(parts):
    return pl.pallas_call(
        unfold_kernel,
        out_shape=jax.ShapeDtypeStruct((27, 32, 32), F32),
        compiler_params=pltpu.CompilerParams(vmem_limit_bytes=4 * MIB),
        name="unfold",
    )(*parts)


def body(volume, cotangent, weights):
    s = lax.axis_index("section")
    l = lax.axis_index("lat")
    pairs = lax.axis_size("lat") // 2
    z = l % 2
    pos = jnp.stack([z, l // 2, s]).astype(jnp.int32)

    def clip(array, at):
        return lax.dynamic_index_in_dim(array, at, 0, keepdims=False)

    same = 2 * s + z
    cross = 2 * s + (1 - z)
    straight = jnp.transpose(weights[0], (2, 3, 4, 0, 1)).reshape(27, 32, 32)
    mine = jnp.stack([straight, jnp.swapaxes(straight, 1, 2)])
    others = permute(mine, other_section)
    v_same, v_cross = clip(volume, same), clip(volume, cross)
    c_same, c_cross = clip(cotangent, same), clip(cotangent, cross)
    near_same = permute(jnp.stack([v_same, c_same]), NEAR_SAME)
    slabs = [
        v_same,
        permute(v_cross, PARTNER),
        permute(v_cross, NEAR_CROSS),
        near_same,
        permute(v_cross, FAR_CROSS),
        permute(v_same, FAR_SAME),
    ]
    c_slabs = [
        c_same,
        permute(c_cross, PARTNER),
        permute(c_cross, NEAR_CROSS),
        near_same,
    ]
    fwd, bwd = make_bands(pos, mine, others)
    xv, xm, pre0, pre1, top_own, top_oth = run_forward(pairs, pos, slabs, fwd)
    d0, keep, send = run_backward(pairs, pos, c_slabs, bwd, xv, xm, pre0, pre1)
    total = keep + permute(send, other_section)
    d0, total = lax.optimization_barrier((d0, total))
    out_own, out_oth = run_last(pos, d0, bwd)
    for axis in (2, 1, 0):
        parts = [total] + [permute(total, ring(axis, step)) for step in (2, 1, 3)]
        if axis:
            total = (parts[0] + parts[1]) + (parts[2] + parts[3])
    at_zero = s == 0
    pieces = [
        out_own,
        top_own,
        permute(jnp.where(at_zero, out_oth, top_oth), PARTNER),
        permute(jnp.where(at_zero, top_own, out_own), other_section),
        permute(jnp.where(at_zero, top_oth, out_oth), other_both),
    ]
    field = run_gather(pos, pieces)
    grads = run_unfold(parts).reshape(3, 3, 3, 32, 32)
    return (field[None], jnp.transpose(grads, (3, 4, 0, 1, 2))[None])


def solution(mesh):
    return jax.shard_map(
        body,
        mesh=mesh,
        in_specs=(
            P("dp", None, "lat", None, None),
            P("dp", None, "lat", None, None),
            P("section", None, None, None, None, None),
        ),
        out_specs=(
            P("section", "dp", None, "lat", None, None),
            P("section", None, None, None, None, None),
        ),
        check_vma=False,
    )
```
